256 devices in a mesh: box: 32 (over x, z), pencil: 8 (over y, core).
Axes of the slice: x: 4, y: 4, z: 8, core: 2. Of those that a mesh axis runs over, the one named last changes fastest.
Arguments:
- previous: bfloat16 [32, 256, 256, 128], P('box', 'pencil'), may hold values from -48 to 48
- source: bfloat16 [32, 256, 256, 128], P('box', 'pencil'), may hold values from -48 to 48
- neighbor: int32 [32, 2, 16], replicated, may hold values from 0 to 31, as said below
- depth: int32 [32, 2, 16], replicated, may hold values from 1 to 8
- wall: int32 [32, 2, 256], P('box', None, 'pencil'), may hold values 0 or 1
Outputs:
- solution: float32 [32, 256, 256, 128], P('box', 'pencil')
The draws below stay inside these ranges and needn't reach their ends.
Inputs may be any that keep to these rules, and one draw needn't show every extreme that they name: For each face and segment, neighbor[:, face, segment] is a permutation of the 32 boxes in which no box names itself.
All inputs are finite; a program needn't handle non-finite values. No bound on the sum of `wall` on one device may be relied on, other than what follows from the above.
Results may differ from the reference program's by a relative error of at most 0.014.
Values may be sent and summed in bfloat16 or wider, within the bound.
A program may use at most 64 MiB of HBM per device.

```python
import jax
import jax.numpy as jnp
from jax import lax

BX = 256
BY = 256
BZ = 128
W = 8
ITERS = 2
NB = 32
NSEG = 16
SEGL = 16


def draw_neighbor(key, part):

    def cycle_draw(subkey):
        ordering = jax.random.permutation(subkey, NB).astype(jnp.int32)
        target = jnp.roll(ordering, -1)
        return jnp.zeros((NB,), jnp.int32).at[ordering].set(target)
    subkeys = jax.random.split(jax.random.fold_in(key, 7), 2 * NSEG)
    table = jax.vmap(cycle_draw)(subkeys)
    return table.reshape(2, NSEG, NB).transpose(2, 0, 1).astype(jnp.int32)


def with_ends(entries, key, least, high):
    shape = entries.shape
    place = [jax.random.randint(jax.random.fold_in(key, axis), (), 0, shape[axis]) for axis in range(len(shape))]
    entries = entries.at[tuple(place)].set(least)
    longest = shape.index(max(shape))
    place[longest] = (place[longest] + 1) % shape[longest]
    return entries.at[tuple(place)].set(high)


def level_of(rng, dims, shards, low, high):
    level = 1.0
    for position, parts in shards:
        steps = jax.random.uniform(jax.random.fold_in(jax.random.fold_in(rng, 6), position), (parts,), jnp.float32, low / len(shards), high / len(shards))
        level = level * jnp.repeat(jnp.exp(steps), dims[position] // parts).reshape((-1,) + (1,) * (len(dims) - 1 - position))
    return level


def centred(key, shape, width, bound, pieces=(), kind=jnp.bfloat16):
    result = jax.random.normal(key, shape, jnp.float32) * width
    if len(pieces) > 0:
        result = level_of(key, shape, pieces, -0.22, 0.18) * result
    return jnp.clip(result, min=-bound, max=bound).astype(kind)


def setup_inputs(seed: int = 0) -> dict:
    keys = jax.random.split(jax.random.key(seed), 6)
    return {
        "previous": centred(keys[0], (NB, BX, BY, BZ), 8.0, 48.0, ((0, 32), (1, 8))),
        "source": centred(keys[1], (NB, BX, BY, BZ), 8.0, 48.0, ((0, 32), (1, 8))),
        "neighbor": draw_neighbor(jax.random.fold_in(keys[5], 71), 0),
        "depth": with_ends(jax.random.randint(keys[3], (NB, 2, NSEG), 1, W + 1), jax.random.fold_in(keys[3], 1), 1, W).astype(jnp.int32),
        "wall": with_ends((jax.random.randint(keys[4], (NB, 2, BX), 0, 4) < 1).astype(jnp.int32), jax.random.fold_in(keys[4], 1), 0, 1),
    }


REFLECT = 0.6
TIMESTEP = 64.0

def sine_table(length):
    ordinal = jnp.arange(length, dtype=jnp.float32) + 1.0
    phase_angle = jnp.pi * ordinal[:, None] * ordinal[None, :] / (length + 1.0)
    return (jnp.sqrt(2.0 / (length + 1.0)) * jnp.sin(phase_angle)).astype(jnp.bfloat16)

def eigen_values(length):
    ordinal = jnp.arange(length, dtype=jnp.float32) + 1.0
    return 2.0 - 2.0 * jnp.cos(jnp.pi * ordinal / (length + 1.0))

def depth_turn(field, table):
    return jnp.einsum('xyz,zk->xyk', field.astype(jnp.float32), table.astype(jnp.float32))

def width_turn(field, table):
    return jnp.einsum('xyz,yk->xkz', field.astype(jnp.float32), table.astype(jnp.float32))

def length_turn(field, table):
    return jnp.einsum('xyz,xk->kyz', field.astype(jnp.float32), table.astype(jnp.float32))

def box_right_side(forcing, current, box_index, neighbor, depth, wall):
    iterate = current[box_index].astype(jnp.float32)
    positions = jnp.arange(BX, dtype=jnp.int32)
    segment = positions // SEGL
    low_donor = neighbor[box_index, 0][segment].astype(jnp.int32)
    high_donor = neighbor[box_index, 1][segment].astype(jnp.int32)
    low_row = (BY - 1 - depth[box_index, 0][segment]).astype(jnp.int32)
    high_row = depth[box_index, 1][segment].astype(jnp.int32)
    low_import = current[low_donor, positions, low_row, :].astype(jnp.float32)
    high_import = current[high_donor, positions, high_row, :].astype(jnp.float32)
    low_ghost = jnp.where(wall[box_index, 0][:, None] == 1, REFLECT * iterate[:, 0, :], low_import)
    high_ghost = jnp.where(wall[box_index, 1][:, None] == 1, REFLECT * iterate[:, BY - 1, :], high_import)
    boundary = jnp.zeros_like(iterate)
    boundary = boundary.at[:, 0, :].add(low_ghost)
    boundary = boundary.at[:, BY - 1, :].add(high_ghost)
    boundary = boundary.at[0].add(REFLECT * iterate[0])
    boundary = boundary.at[BX - 1].add(REFLECT * iterate[BX - 1])
    boundary = boundary.at[:, :, 0].add(REFLECT * iterate[:, :, 0])
    boundary = boundary.at[:, :, BZ - 1].add(REFLECT * iterate[:, :, BZ - 1])
    return (forcing + TIMESTEP * boundary).astype(jnp.bfloat16)

def reference(previous, source, neighbor, depth, wall):
    length_table = sine_table(BX)
    width_table = sine_table(BY)
    depth_table = sine_table(BZ)
    spectrum = 1.0 + TIMESTEP * (eigen_values(BX)[:, None, None] + eigen_values(BY)[None, :, None] + eigen_values(BZ)[None, None, :])
    current = previous
    solved = None
    for iteration in range(ITERS):

        def one_box(box_index, current=current):
            forcing = previous[box_index].astype(jnp.float32) + source[box_index].astype(jnp.float32)
            right_side = box_right_side(forcing, current, box_index, neighbor, depth, wall)
            first_pass = depth_turn(right_side, depth_table).astype(jnp.bfloat16)
            second_pass = width_turn(first_pass, width_table).astype(jnp.bfloat16)
            third_pass = length_turn(second_pass, length_table)
            fourth_pass = (third_pass / spectrum).astype(jnp.bfloat16)
            fifth_pass = length_turn(fourth_pass, length_table).astype(jnp.bfloat16)
            sixth_pass = width_turn(fifth_pass, width_table).astype(jnp.bfloat16)
            return depth_turn(sixth_pass, depth_table)
        solved = lax.map(one_box, jnp.arange(NB, dtype=jnp.int32))
        current = solved.astype(jnp.bfloat16)
    return solved
```

```python
import functools

import jax
import jax.numpy as jnp
import ml_dtypes
import numpy as np
from jax import lax
from jax.experimental import pallas as pl
from jax.experimental.pallas import tpu as pltpu
from jax.sharding import PartitionSpec as P

W = 8
REFLECT = 0.6
TIMESTEP = 64.0
ZCHIPS = 8
SLAB = 16
CHUNK = 32
LOADS = 8

BF16 = ml_dtypes.bfloat16


def sine_table(length):
    ordinal = np.arange(length, dtype=np.float64) + 1.0
    phase_angle = np.pi * ordinal[:, None] * ordinal[None, :] / (length + 1.0)
    return np.sqrt(2.0 / (length + 1.0)) * np.sin(phase_angle)


def eigen_values(length):
    ordinal = np.arange(length, dtype=np.float64) + 1.0
    return 2.0 - 2.0 * np.cos(np.pi * ordinal / (length + 1.0))


def constants(planes, columns, heights):
    width = sine_table(columns)
    height = sine_table(heights).astype(BF16).astype(np.float64)
    gain = TIMESTEP * REFLECT
    faces = np.zeros((heights, heights))
    faces[0] = gain * height[0]
    faces[-1] = gain * height[-1]
    both = np.block([[height, height], [faces, np.zeros_like(faces)]])
    turn = gain * (np.outer(height[:, 0], height[0]) + np.outer(height[:, -1], height[-1]))
    nothing = np.zeros_like(turn)
    turns = np.block([[turn, nothing], [nothing, turn]])
    heights_two = np.block([[height, nothing], [nothing, height]])
    rows = np.concatenate([width[: W + 1], width[-W - 1 :]])
    rows = np.pad(rows, ((0, (-len(rows)) % 8), (0, 0)))
    slope = 2.0 + 1.0 / TIMESTEP + eigen_values(columns)[:, None] + eigen_values(heights)[None, :]
    ratio = 2.0 / (slope + np.sqrt(slope * slope - 4.0))
    weight = ratio / (1.0 - ratio * ratio) / TIMESTEP
    edge = np.broadcast_to(TIMESTEP * width[0][:, None], ratio.shape)
    modes = np.stack([ratio, planes * np.log(ratio), weight, edge])
    return dict(
        width=width.astype(BF16),
        height=height.astype(BF16),
        both=both.astype(BF16),
        turns=turns.astype(BF16),
        heights_two=heights_two.astype(BF16),
        rows=rows.astype(np.float32),
        modes=modes.astype(np.float32),
    )


def front_kernel(
    pencils, previous, source, neighbor, depth, wall, width, height, both, turns, rowtab, modes,
    out, prev, src, slab, right, force, carry, iterate, waves, inbox, own, gath0, gath1, packet, zbox0, zbox1,
    rows, ghost, walls, picks, load_sem, slab_sem, out_sem, x_send, x_recv, z_send, z_recv,
    w_send, w_recv,
):
    gath = (gath0, gath1)
    zbox = (zbox0, zbox1)
    planes, columns, heights = prev.shape
    pencil = lax.axis_index("pencil")
    box = lax.axis_index("box")
    boxes = neighbor.shape[0]
    xchips = boxes // ZCHIPS
    cx = box // ZCHIPS
    cz = box % ZCHIPS
    seglen = planes * pencils // neighbor.shape[2]
    segs = planes // seglen
    gain = TIMESTEP * REFLECT
    step = planes // LOADS

    x_peers = [(lax.rem(cx + k, xchips)) * ZCHIPS + cz for k in range(1, xchips)]
    z_peers = [cx * ZCHIPS + lax.rem(cz + k, ZCHIPS) for k in range(1, ZCHIPS)]
    w_peers = [lax.rem(pencil + k, pencils) for k in range(1, pencils)]

    barrier = pltpu.get_barrier_semaphore()
    for peer in x_peers + z_peers:
        pl.semaphore_signal(barrier, inc=1, device_id=(peer, pencil), device_id_type=pl.DeviceIdType.MESH)
    for peer in w_peers:
        pl.semaphore_signal(barrier, inc=1, device_id=(box, peer), device_id_type=pl.DeviceIdType.MESH)

    slab_loads = [
        pltpu.make_async_copy(previous.at[:, pl.ds(0, SLAB), :], slab.at[0], slab_sem.at[0]),
        pltpu.make_async_copy(previous.at[:, pl.ds(columns - SLAB, SLAB), :], slab.at[1], slab_sem.at[1]),
    ]
    for load in slab_loads:
        load.start()
    loads = []
    for c in range(LOADS):
        part = pl.ds(c * step, step)
        loads.append((
            pltpu.make_async_copy(previous.at[part], prev.at[part], load_sem.at[0, c]),
            pltpu.make_async_copy(source.at[part], src.at[part], load_sem.at[1, c]),
        ))
        loads[-1][0].start()
        loads[-1][1].start()

    lists = [(f, t) for f in range(2) for t in range(segs)]

    def search(b, found):
        return tuple(
            jnp.where(neighbor[b, f, pencil * segs + t] == box, depth[b, f, pencil * segs + t], d)
            for (f, t), d in zip(lists, found)
        )

    depths = lax.fori_loop(0, boxes, search, tuple(jnp.int32(1) for _ in lists))

    line = lax.broadcasted_iota(jnp.int32, (planes, heights), 0)
    for f in range(2):
        def mark(x, mask, f=f):
            return jnp.where(line == x, wall[f, x], mask)

        walls[f] = lax.fori_loop(0, planes, mark, jnp.zeros((planes, heights), jnp.int32))

    def x_copies(it):
        return [
            pltpu.make_async_remote_copy(
                gath[it].at[0], gath[it].at[k], x_send.at[it, k - 1], x_recv.at[it, k - 1],
                device_id=(x_peers[k - 1], pencil), device_id_type=pl.DeviceIdType.MESH,
            )
            for k in range(1, xchips)
        ]

    def z_copies(it):
        return [
            pltpu.make_async_remote_copy(
                packet.at[it, k - 1], zbox[it].at[k], z_send.at[it, k - 1], z_recv.at[it, k - 1],
                device_id=(z_peers[k - 1], pencil), device_id_type=pl.DeviceIdType.MESH,
            )
            for k in range(1, ZCHIPS)
        ]

    def w_copies(it):
        return [
            pltpu.make_async_remote_copy(
                waves.at[it, (pencil + k) // pencils], inbox.at[it, k - 1],
                w_send.at[it, k - 1], w_recv.at[it, k - 1],
                device_id=(box, w_peers[k - 1]), device_id_type=pl.DeviceIdType.MESH,
            )
            for k in range(1, pencils)
        ]

    def forward_margins(it):
        for k in range(ZCHIPS):
            reader = box if k == 0 else z_peers[k - 1]
            for j, (f, t) in enumerate(lists):
                donor = neighbor[reader, f, pencil * segs + t]
                block = gath[it][lax.rem(cx - donor // ZCHIPS + xchips, xchips), j]
                if k == 0:
                    zbox[it][0, j] = block
                else:
                    packet[it, k - 1, j] = block

    def imported(it, j):
        f, t = lists[j]
        donor = neighbor[box, f, pencil * segs + t]
        return zbox[it][lax.rem(cz - lax.rem(donor, ZCHIPS) + ZCHIPS, ZCHIPS), j].astype(jnp.float32)

    def imports(it, f):
        return jnp.concatenate([imported(it, f * segs + t) for t in range(segs)], axis=0)

    for load in slab_loads:
        load.wait()
    place = lax.broadcasted_iota(jnp.int32, (seglen, SLAB, heights), 1)
    for j, (f, t) in enumerate(lists):
        row = SLAB - 1 - depths[j] if f == 0 else depths[j]
        near = slab[1 - f, pl.ds(t * seglen, seglen)].astype(jnp.float32)
        gath0[0, j] = jnp.sum(jnp.where(place == row, near, 0.0), axis=1).astype(jnp.bfloat16)
    pl.semaphore_wait(barrier, len(x_peers) + len(z_peers) + len(w_peers))
    first_x = x_copies(0)
    for copy in first_x:
        copy.start()

    def transform(x, _):
        now = prev[x]
        total = (now.astype(jnp.float32) + src[x].astype(jnp.float32)).astype(jnp.bfloat16)
        turned = jnp.dot(
            width[...], jnp.concatenate([total, now], axis=1), preferred_element_type=jnp.float32
        ).astype(jnp.bfloat16)
        result = jnp.dot(turned, both[...], preferred_element_type=jnp.float32)
        right[x] = result[:, :heights]
        force[x] = result[:, heights:]
        return 0

    first_z = z_copies(0)
    for c in range(LOADS):
        for load in loads[c]:
            load.wait()
        lax.fori_loop(c * step, (c + 1) * step, transform, 0)
        if c == LOADS // 2 - 1:
            for copy in first_x:
                copy.wait_recv()
            forward_margins(0)
            for copy in first_z:
                copy.start()

    at_start = jnp.where(pencil == 0, gain, 0.0).astype(jnp.float32)
    at_end = jnp.where(pencil == pencils - 1, gain, 0.0).astype(jnp.float32)
    for x, scale in ((0, at_start), (planes - 1, at_end)):
        turned = jnp.dot(width[...], prev[x], preferred_element_type=jnp.float32).astype(jnp.bfloat16)
        right[x] += scale * jnp.dot(turned, height[...], preferred_element_type=jnp.float32)

    for copy in first_z:
        copy.wait_recv()
    for f in range(2):
        wallrow = slab[f, :, 0 if f == 0 else SLAB - 1, :].astype(jnp.float32)
        value = jnp.where(walls[f] == 1, REFLECT * wallrow, imports(0, f))
        ghost[f] = jnp.dot(value.astype(jnp.bfloat16), height[...], preferred_element_type=jnp.float32)

    parity = lax.broadcasted_iota(jnp.int32, (CHUNK, heights), 0) % 2
    sign = jnp.where(parity == 0, 1.0, -1.0).astype(jnp.float32)
    near_power = (2 * pencil + 1).astype(jnp.float32)
    far_power = (2 * pencils - 1 - 2 * pencil).astype(jnp.float32)

    def chunk_at(c):
        return pl.ds(pl.multiple_of(c * CHUNK, CHUNK), CHUNK)

    def sweep(it):
        def chunk(c, _):
            at = chunk_at(c)
            ratio = modes[0, at]
            edge = modes[3, at]

            def plane(i, carried):
                up, down, power = carried
                reach = ghost[0, pl.ds(i, 1), :] + sign * ghost[1, pl.ds(i, 1), :]
                value = right[i, at] + edge * reach
                right[i, at] = value
                return value + ratio * up, down + power * value, power * ratio

            zero = jnp.zeros((CHUNK, heights), jnp.float32)
            up, down, _ = lax.fori_loop(0, planes, plane, (zero, zero, zero + 1.0), unroll=4)
            log = modes[1, at]
            waves[it, 0, at] = (up - ratio * jnp.exp(log * near_power) * down).astype(jnp.bfloat16)
            waves[it, 1, at] = (down - ratio * jnp.exp(log * far_power) * up).astype(jnp.bfloat16)
            loop = ratio * ratio * jnp.exp(log * (2 * pencils - 1))
            own[0, at] = loop * up - ratio * jnp.exp(log * (near_power - 1.0)) * down
            own[1, at] = loop * down - ratio * jnp.exp(log * (far_power - 1.0)) * up
            return 0

        lax.fori_loop(0, columns // CHUNK, chunk, 0)

    def solve(it, done=None):
        def chunk(c, _):
            at = chunk_at(c)
            ratio = modes[0, at]
            log = modes[1, at]
            weight = modes[2, at]
            decay = jnp.exp(log)
            low = jnp.zeros((CHUNK, heights), jnp.float32)
            high = low
            for k in range(pencils - 1, 0, -1):
                here = jnp.where(pencil >= k, 1.0, 0.0).astype(jnp.float32)
                low = here * inbox[it, k - 1, at].astype(jnp.float32) + decay * low
            for k in range(1, pencils):
                here = jnp.where(pencil >= k, 0.0, 1.0).astype(jnp.float32)
                high = here * inbox[it, k - 1, at].astype(jnp.float32) + decay * high
            start = low + own[0, at] - ratio * jnp.exp(log * near_power) * high
            end = high + own[1, at] - ratio * jnp.exp(log * far_power) * low

            def rising(i, value):
                value = right[i, at] + ratio * value
                carry[i, at] = value
                return value

            lax.fori_loop(0, planes, rising, start, unroll=4)

            def falling(j, value):
                i = planes - 1 - j
                value = ratio * value
                iterate[i, at] = (weight * (carry[i, at] + value)).astype(jnp.bfloat16)
                return value + right[i, at]

            lax.fori_loop(0, planes, falling, end, unroll=4)
            if done is not None:
                done(c, at)
            return 0

        lax.fori_loop(0, columns // CHUNK, chunk, 0)

    sweep(0)
    first_w = w_copies(0)
    for copy in first_w:
        copy.start()
    for copy in first_w:
        copy.wait_recv()
    solve(0)

    picks[...] = jnp.zeros_like(picks)
    for t in range(segs):
        low_row = 2 * W + 1 - depths[t]
        high_row = depths[segs + t]
        for q, row in enumerate((0, 2 * W + 1, low_row, high_row)):
            picks[t, pl.ds(q, 1), :] = rowtab[pl.ds(row, 1), :]

    def pair_of(j):
        return jnp.concatenate([iterate[2 * j], iterate[2 * j + 1]], axis=1)

    for t in range(segs):
        lhs = picks[t].astype(jnp.bfloat16)

        def take(j, _):
            taken = jnp.dot(lhs, pair_of(j), preferred_element_type=jnp.float32)
            for q in range(4):
                rows[q, pl.ds(2 * j, 1), :] = taken[q : q + 1, :heights]
                rows[q, pl.ds(2 * j + 1, 1), :] = taken[q : q + 1, heights:]
            return 0

        lax.fori_loop(t * seglen // 2, (t + 1) * seglen // 2, take, 0)
    for j, (f, t) in enumerate(lists):
        gath1[0, j] = rows[2 + f, pl.ds(t * seglen, seglen), :].astype(jnp.bfloat16)
    second_x = x_copies(1)
    for copy in second_x:
        copy.start()

    def faces(j, _):
        added = jnp.dot(pair_of(j), turns[...], preferred_element_type=jnp.float32)
        right[2 * j] = force[2 * j] + added[:, :heights]
        right[2 * j + 1] = force[2 * j + 1] + added[:, heights:]
        return 0

    lax.fori_loop(0, planes // 4, faces, 0)
    for copy in second_x:
        copy.wait_recv()
    forward_margins(1)
    second_z = z_copies(1)
    for copy in second_z:
        copy.start()
    lax.fori_loop(planes // 4, planes // 2, faces, 0)
    right[0] += at_start * iterate[0].astype(jnp.float32)
    right[planes - 1] += at_end * iterate[planes - 1].astype(jnp.float32)
    for copy in second_z:
        copy.wait_recv()
    for f in range(2):
        ghost[f] = jnp.where(walls[f] == 1, REFLECT * rows[f], imports(1, f))

    sweep(1)
    second_w = w_copies(1)
    for copy in second_w:
        copy.start()
    for copy in second_w:
        copy.wait_recv()

    def store(c, at):
        pltpu.make_async_copy(iterate.at[:, at, :], out.at[:, at, :], out_sem.at[c]).start()

    solve(1, store)
    for c in range(columns // CHUNK):
        at = pl.ds(c * CHUNK, CHUNK)
        pltpu.make_async_copy(iterate.at[:, at, :], out.at[:, at, :], out_sem.at[c]).wait()
    for copy in first_x + first_z + first_w + second_x + second_z + second_w:
        copy.wait_send()


def back_kernel(modes, width, heights_two, solved):
    planes, _, heights = modes.shape
    for j in range(planes // 2):
        pair = jnp.concatenate([modes[2 * j], modes[2 * j + 1]], axis=1)
        half = jnp.dot(pair, heights_two[...], preferred_element_type=jnp.float32).astype(jnp.bfloat16)
        full = jnp.dot(width[...], half, preferred_element_type=jnp.float32)
        solved[2 * j] = full[:, :heights]
        solved[2 * j + 1] = full[:, heights:]


def shards(previous, source, neighbor, depth, wall):
    pencils = lax.axis_size("pencil")
    _, planes, columns, heights = previous.shape
    boxes, _, segments = neighbor.shape
    segs = planes * segments // (planes * pencils)
    seglen = planes // segs
    xchips = boxes // ZCHIPS
    table = {name: jnp.asarray(value) for name, value in constants(planes, columns, heights).items()}
    lists = 2 * segs
    field = (planes, columns, heights)
    block = (seglen, heights)
    vmem = pl.BlockSpec(memory_space=pltpu.VMEM)
    smem = pl.BlockSpec(memory_space=pltpu.SMEM)
    far = pl.BlockSpec(memory_space=pl.ANY)
    dma = pltpu.SemaphoreType.DMA
    modes = pl.pallas_call(
        functools.partial(front_kernel, pencils),
        out_shape=jax.ShapeDtypeStruct(field, jnp.bfloat16),
        in_specs=[far, far, smem, smem, smem] + [vmem] * 6,
        out_specs=far,
        scratch_shapes=[
            pltpu.VMEM(field, jnp.bfloat16),
            pltpu.VMEM(field, jnp.bfloat16),
            pltpu.VMEM((2, planes, SLAB, heights), jnp.bfloat16),
            pltpu.VMEM(field, jnp.float32),
            pltpu.VMEM(field, jnp.float32),
            pltpu.VMEM(field, jnp.float32),
            pltpu.VMEM(field, jnp.bfloat16),
            pltpu.VMEM((2, 2, columns, heights), jnp.bfloat16),
            pltpu.VMEM((2, pencils - 1, columns, heights), jnp.bfloat16),
            pltpu.VMEM((2, columns, heights), jnp.float32),
            pltpu.VMEM((xchips, lists) + block, jnp.bfloat16),
            pltpu.VMEM((xchips, lists) + block, jnp.bfloat16),
            pltpu.VMEM((2, ZCHIPS - 1, lists) + block, jnp.bfloat16),
            pltpu.VMEM((ZCHIPS, lists) + block, jnp.bfloat16),
            pltpu.VMEM((ZCHIPS, lists) + block, jnp.bfloat16),
            pltpu.VMEM((4, planes, heights), jnp.float32),
            pltpu.VMEM((2, planes, heights), jnp.float32),
            pltpu.VMEM((2, planes, heights), jnp.int32),
            pltpu.VMEM((segs, 8, columns), jnp.float32),
            dma((2, LOADS)),
            dma((2,)),
            dma((columns // CHUNK,)),
            dma((2, xchips - 1)),
            dma((2, xchips - 1)),
            dma((2, ZCHIPS - 1)),
            dma((2, ZCHIPS - 1)),
            dma((2, pencils - 1)),
            dma((2, pencils - 1)),
        ],
        compiler_params=pltpu.CompilerParams(
            collective_id=0, has_side_effects=True, vmem_limit_bytes=40 * 1024 * 1024
        ),
        name="schwarz_modes",
    )(
        previous[0], source[0], neighbor, depth, wall[0],
        table["width"], table["height"], table["both"], table["turns"], table["rows"], table["modes"],
    )
    group = 4
    solved = pl.pallas_call(
        back_kernel,
        out_shape=jax.ShapeDtypeStruct(field, jnp.float32),
        grid=(planes // group,),
        in_specs=[
            pl.BlockSpec((group, columns, heights), lambda i: (i, 0, 0)),
            pl.BlockSpec((columns, columns), lambda i: (0, 0)),
            pl.BlockSpec((2 * heights, 2 * heights), lambda i: (0, 0)),
        ],
        out_specs=pl.BlockSpec((group, columns, heights), lambda i: (i, 0, 0)),
        name="back_to_cells",
    )(modes, table["width"], table["heights_two"])
    return solved[None]


def solution(mesh):
    placed = (
        P("box", "pencil", None, None),
        P("box", "pencil", None, None),
        P(),
        P(),
        P("box", None, "pencil"),
    )
    return jax.shard_map(
        shards,
        mesh=mesh,
        in_specs=placed,
        out_specs=P("box", "pencil", None, None),
        check_vma=False,
    )
```

```python
import functools

import jax
import jax.numpy as jnp
import ml_dtypes
import numpy as np
from jax import lax
from jax.experimental import pallas as pl
from jax.experimental.pallas import tpu as pltpu
from jax.sharding import PartitionSpec as P

W = 8
REFLECT = 0.6
TIMESTEP = 64.0
ZCHIPS = 8
SLAB = 16
CHUNK = 32
LOADS = 8

BF16 = ml_dtypes.bfloat16


def sine_table(length):
    ordinal = np.arange(length, dtype=np.float64) + 1.0
    phase_angle = np.pi * ordinal[:, None] * ordinal[None, :] / (length + 1.0)
    return np.sqrt(2.0 / (length + 1.0)) * np.sin(phase_angle)


def eigen_values(length):
    ordinal = np.arange(length, dtype=np.float64) + 1.0
    return 2.0 - 2.0 * np.cos(np.pi * ordinal / (length + 1.0))


def constants(planes, columns, heights):
    width = sine_table(columns)
    height = sine_table(heights).astype(BF16).astype(np.float64)
    gain = TIMESTEP * REFLECT
    faces = np.zeros((heights, heights))
    faces[0] = gain * height[0]
    faces[-1] = gain * height[-1]
    both = np.block([[height, height], [faces, np.zeros_like(faces)]])
    turn = gain * (np.outer(height[:, 0], height[0]) + np.outer(height[:, -1], height[-1]))
    nothing = np.zeros_like(turn)
    turns = np.block([[turn, nothing], [nothing, turn]])
    heights_two = np.block([[height, nothing], [nothing, height]])
    rows = np.concatenate([width[: W + 1], width[-W - 1 :]])
    rows = np.pad(rows, ((0, (-len(rows)) % 8), (0, 0)))
    slope = 2.0 + 1.0 / TIMESTEP + eigen_values(columns)[:, None] + eigen_values(heights)[None, :]
    ratio = 2.0 / (slope + np.sqrt(slope * slope - 4.0))
    weight = ratio / (1.0 - ratio * ratio) / TIMESTEP
    edge = np.broadcast_to(TIMESTEP * width[0][:, None], ratio.shape)
    modes = np.stack([ratio, planes * np.log(ratio), weight, edge])
    return dict(
        width=width.astype(BF16),
        height=height.astype(BF16),
        both=both.astype(BF16),
        turns=turns.astype(BF16),
        heights_two=heights_two.astype(BF16),
        rows=rows.astype(np.float32),
        modes=modes.astype(np.float32),
    )


def front_kernel(
    pencils, previous, source, neighbor_far, depth_far, wall_far, *more
):
    tables_far, (out, neighbor, depth, wall), more = more[:6], more[6:10], more[10:]
    tables, more = more[:6], more[6:]
    width, height, both, turns, rowtab, modes = tables
    run_front(
        pencils, previous, source, (neighbor_far, depth_far, wall_far) + tables_far,
        (neighbor, depth, wall) + tables, *tables, neighbor, depth, wall, out, *more
    )


def run_front(
    pencils, previous, source, smalls_far, smalls, width, height, both, turns, rowtab, modes,
    neighbor, depth, wall,
    out, prev, src, slab, right, force, carry, iterate, waves, inbox, own, gath0, gath1, packet, zbox0, zbox1,
    rows, ghost, walls, picks, load_sem, slab_sem, small_sem, out_sem, x_send, x_recv, z_send, z_recv,
    w_send, w_recv,
):
    gath = (gath0, gath1)
    zbox = (zbox0, zbox1)
    planes, columns, heights = prev.shape
    pencil = lax.axis_index("pencil")
    box = lax.axis_index("box")
    boxes = neighbor.shape[2]
    xchips = boxes // ZCHIPS
    cx = box // ZCHIPS
    cz = box % ZCHIPS
    seglen = planes * pencils // neighbor.shape[1]
    segs = planes // seglen
    gain = TIMESTEP * REFLECT
    step = planes // LOADS

    x_peers = [(lax.rem(cx + k, xchips)) * ZCHIPS + cz for k in range(1, xchips)]
    z_peers = [cx * ZCHIPS + lax.rem(cz + k, ZCHIPS) for k in range(1, ZCHIPS)]
    w_peers = [lax.rem(pencil + k, pencils) for k in range(1, pencils)]

    barrier = pltpu.get_barrier_semaphore()
    for peer in x_peers + z_peers:
        pl.semaphore_signal(barrier, inc=1, device_id=(peer, pencil), device_id_type=pl.DeviceIdType.MESH)
    for peer in w_peers:
        pl.semaphore_signal(barrier, inc=1, device_id=(box, peer), device_id_type=pl.DeviceIdType.MESH)

    slab_loads = [
        pltpu.make_async_copy(previous.at[:, pl.ds(0, SLAB), :], slab.at[0], slab_sem.at[0]),
        pltpu.make_async_copy(previous.at[:, pl.ds(columns - SLAB, SLAB), :], slab.at[1], slab_sem.at[1]),
    ]
    small_loads = [
        pltpu.make_async_copy(there, here, small_sem.at[i])
        for i, (there, here) in enumerate(zip(smalls_far, smalls))
    ]
    for load in slab_loads + small_loads:
        load.start()
    loads = []
    for c in range(LOADS):
        part = pl.ds(c * step, step)
        loads.append((
            pltpu.make_async_copy(previous.at[part], prev.at[part], load_sem.at[0, c]),
            pltpu.make_async_copy(source.at[part], src.at[part], load_sem.at[1, c]),
        ))
        loads[-1][0].start()
        loads[-1][1].start()

    for load in small_loads:
        load.wait()
    lists = [(f, t) for f in range(2) for t in range(segs)]

    def search(b, found):
        return tuple(
            jnp.where(neighbor[f, pencil * segs + t, b] == box, depth[f, pencil * segs + t, b], d)
            for (f, t), d in zip(lists, found)
        )

    depths = lax.fori_loop(0, boxes, search, tuple(jnp.int32(1) for _ in lists))

    line = lax.broadcasted_iota(jnp.int32, (planes, heights), 0)
    for f in range(2):
        def mark(x, mask, f=f):
            return jnp.where(line == x, wall[f, x], mask)

        walls[f] = lax.fori_loop(0, planes, mark, jnp.zeros((planes, heights), jnp.int32))

    def x_copies(it):
        return [
            pltpu.make_async_remote_copy(
                gath[it].at[0], gath[it].at[k], x_send.at[it, k - 1], x_recv.at[it, k - 1],
                device_id=(x_peers[k - 1], pencil), device_id_type=pl.DeviceIdType.MESH,
            )
            for k in range(1, xchips)
        ]

    def z_copies(it):
        return [
            pltpu.make_async_remote_copy(
                packet.at[it, k - 1], zbox[it].at[k], z_send.at[it, k - 1], z_recv.at[it, k - 1],
                device_id=(z_peers[k - 1], pencil), device_id_type=pl.DeviceIdType.MESH,
            )
            for k in range(1, ZCHIPS)
        ]

    def w_copies(it):
        return [
            pltpu.make_async_remote_copy(
                waves.at[it, (pencil + k) // pencils], inbox.at[it, k - 1],
                w_send.at[it, k - 1], w_recv.at[it, k - 1],
                device_id=(box, w_peers[k - 1]), device_id_type=pl.DeviceIdType.MESH,
            )
            for k in range(1, pencils)
        ]

    def forward_margins(it):
        for k in range(ZCHIPS):
            reader = box if k == 0 else z_peers[k - 1]
            for j, (f, t) in enumerate(lists):
                donor = neighbor[f, pencil * segs + t, reader]
                block = gath[it][lax.rem(cx - donor // ZCHIPS + xchips, xchips), j]
                if k == 0:
                    zbox[it][0, j] = block
                else:
                    packet[it, k - 1, j] = block

    def imported(it, j):
        f, t = lists[j]
        donor = neighbor[f, pencil * segs + t, box]
        return zbox[it][lax.rem(cz - lax.rem(donor, ZCHIPS) + ZCHIPS, ZCHIPS), j].astype(jnp.float32)

    def imports(it, f):
        return jnp.concatenate([imported(it, f * segs + t) for t in range(segs)], axis=0)

    for load in slab_loads:
        load.wait()
    place = lax.broadcasted_iota(jnp.int32, (seglen, SLAB, heights), 1)
    for j, (f, t) in enumerate(lists):
        row = SLAB - 1 - depths[j] if f == 0 else depths[j]
        near = slab[1 - f, pl.ds(t * seglen, seglen)].astype(jnp.float32)
        gath0[0, j] = jnp.sum(jnp.where(place == row, near, 0.0), axis=1).astype(jnp.bfloat16)
    pl.semaphore_wait(barrier, len(x_peers) + len(z_peers) + len(w_peers))
    first_x = x_copies(0)
    for copy in first_x:
        copy.start()

    def transform(x, _):
        now = prev[x]
        total = (now.astype(jnp.float32) + src[x].astype(jnp.float32)).astype(jnp.bfloat16)
        turned = jnp.dot(
            width[...], jnp.concatenate([total, now], axis=1), preferred_element_type=jnp.float32
        ).astype(jnp.bfloat16)
        result = jnp.dot(turned, both[...], preferred_element_type=jnp.float32)
        right[x] = result[:, :heights]
        force[x] = result[:, heights:]
        return 0

    first_z = z_copies(0)
    for c in range(LOADS):
        for load in loads[c]:
            load.wait()
        lax.fori_loop(c * step, (c + 1) * step, transform, 0)
        if c == LOADS // 2 - 1:
            for copy in first_x:
                copy.wait_recv()
            forward_margins(0)
            for copy in first_z:
                copy.start()

    at_start = jnp.where(pencil == 0, gain, 0.0).astype(jnp.float32)
    at_end = jnp.where(pencil == pencils - 1, gain, 0.0).astype(jnp.float32)
    for x, scale in ((0, at_start), (planes - 1, at_end)):
        turned = jnp.dot(width[...], prev[x], preferred_element_type=jnp.float32).astype(jnp.bfloat16)
        right[x] += scale * jnp.dot(turned, height[...], preferred_element_type=jnp.float32)

    for copy in first_z:
        copy.wait_recv()
    for f in range(2):
        wallrow = slab[f, :, 0 if f == 0 else SLAB - 1, :].astype(jnp.float32)
        value = jnp.where(walls[f] == 1, REFLECT * wallrow, imports(0, f))
        ghost[f] = jnp.dot(value.astype(jnp.bfloat16), height[...], preferred_element_type=jnp.float32)

    parity = lax.broadcasted_iota(jnp.int32, (CHUNK, heights), 0) % 2
    sign = jnp.where(parity == 0, 1.0, -1.0).astype(jnp.float32)
    near_power = (2 * pencil + 1).astype(jnp.float32)
    far_power = (2 * pencils - 1 - 2 * pencil).astype(jnp.float32)

    def chunk_at(c):
        return pl.ds(pl.multiple_of(c * CHUNK, CHUNK), CHUNK)

    def sweep(it):
        def chunk(c, _):
            at = chunk_at(c)
            ratio = modes[0, at]
            edge = modes[3, at]

            def plane(i, carried):
                up, down, power = carried
                reach = ghost[0, pl.ds(i, 1), :] + sign * ghost[1, pl.ds(i, 1), :]
                value = right[i, at] + edge * reach
                right[i, at] = value
                return value + ratio * up, down + power * value, power * ratio

            zero = jnp.zeros((CHUNK, heights), jnp.float32)
            up, down, _ = lax.fori_loop(0, planes, plane, (zero, zero, zero + 1.0), unroll=4)
            log = modes[1, at]
            waves[it, 0, at] = (up - ratio * jnp.exp(log * near_power) * down).astype(jnp.bfloat16)
            waves[it, 1, at] = (down - ratio * jnp.exp(log * far_power) * up).astype(jnp.bfloat16)
            loop = ratio * ratio * jnp.exp(log * (2 * pencils - 1))
            own[0, at] = loop * up - ratio * jnp.exp(log * (near_power - 1.0)) * down
            own[1, at] = loop * down - ratio * jnp.exp(log * (far_power - 1.0)) * up
            return 0

        lax.fori_loop(0, columns // CHUNK, chunk, 0)

    def solve(it, done=None):
        def chunk(c, _):
            at = chunk_at(c)
            ratio = modes[0, at]
            log = modes[1, at]
            weight = modes[2, at]
            decay = jnp.exp(log)
            low = jnp.zeros((CHUNK, heights), jnp.float32)
            high = low
            for k in range(pencils - 1, 0, -1):
                here = jnp.where(pencil >= k, 1.0, 0.0).astype(jnp.float32)
                low = here * inbox[it, k - 1, at].astype(jnp.float32) + decay * low
            for k in range(1, pencils):
                here = jnp.where(pencil >= k, 0.0, 1.0).astype(jnp.float32)
                high = here * inbox[it, k - 1, at].astype(jnp.float32) + decay * high
            start = low + own[0, at] - ratio * jnp.exp(log * near_power) * high
            end = high + own[1, at] - ratio * jnp.exp(log * far_power) * low

            def rising(i, value):
                value = right[i, at] + ratio * value
                carry[i, at] = value
                return value

            lax.fori_loop(0, planes, rising, start, unroll=4)

            def falling(j, value):
                i = planes - 1 - j
                value = ratio * value
                iterate[i, at] = (weight * (carry[i, at] + value)).astype(jnp.bfloat16)
                return value + right[i, at]

            lax.fori_loop(0, planes, falling, end, unroll=4)
            if done is not None:
                done(c, at)
            return 0

        lax.fori_loop(0, columns // CHUNK, chunk, 0)

    sweep(0)
    first_w = w_copies(0)
    for copy in first_w:
        copy.start()
    for copy in first_w:
        copy.wait_recv()
    solve(0)

    picks[...] = jnp.zeros_like(picks)
    for t in range(segs):
        low_row = 2 * W + 1 - depths[t]
        high_row = depths[segs + t]
        for q, row in enumerate((0, 2 * W + 1, low_row, high_row)):
            picks[t, pl.ds(q, 1), :] = rowtab[pl.ds(row, 1), :]

    def pair_of(j):
        return jnp.concatenate([iterate[2 * j], iterate[2 * j + 1]], axis=1)

    for t in range(segs):
        lhs = picks[t].astype(jnp.bfloat16)

        def take(j, _):
            taken = jnp.dot(lhs, pair_of(j), preferred_element_type=jnp.float32)
            for q in range(4):
                rows[q, pl.ds(2 * j, 1), :] = taken[q : q + 1, :heights]
                rows[q, pl.ds(2 * j + 1, 1), :] = taken[q : q + 1, heights:]
            return 0

        lax.fori_loop(t * seglen // 2, (t + 1) * seglen // 2, take, 0)
    for j, (f, t) in enumerate(lists):
        gath1[0, j] = rows[2 + f, pl.ds(t * seglen, seglen), :].astype(jnp.bfloat16)
    second_x = x_copies(1)
    for copy in second_x:
        copy.start()

    def faces(j, _):
        added = jnp.dot(pair_of(j), turns[...], preferred_element_type=jnp.float32)
        right[2 * j] = force[2 * j] + added[:, :heights]
        right[2 * j + 1] = force[2 * j + 1] + added[:, heights:]
        return 0

    lax.fori_loop(0, planes // 4, faces, 0)
    for copy in second_x:
        copy.wait_recv()
    forward_margins(1)
    second_z = z_copies(1)
    for copy in second_z:
        copy.start()
    lax.fori_loop(planes // 4, planes // 2, faces, 0)
    right[0] += at_start * iterate[0].astype(jnp.float32)
    right[planes - 1] += at_end * iterate[planes - 1].astype(jnp.float32)
    for copy in second_z:
        copy.wait_recv()
    for f in range(2):
        ghost[f] = jnp.where(walls[f] == 1, REFLECT * rows[f], imports(1, f))

    sweep(1)
    second_w = w_copies(1)
    for copy in second_w:
        copy.start()
    for copy in second_w:
        copy.wait_recv()

    def store(c, at):
        pltpu.make_async_copy(iterate.at[:, at, :], out.at[:, at, :], out_sem.at[c]).start()

    solve(1, store)
    for c in range(columns // CHUNK):
        at = pl.ds(c * CHUNK, CHUNK)
        pltpu.make_async_copy(iterate.at[:, at, :], out.at[:, at, :], out_sem.at[c]).wait()
    for copy in first_x + first_z + first_w + second_x + second_z + second_w:
        copy.wait_send()


def back_kernel(modes, width, heights_two, solved):
    planes, _, heights = modes.shape
    for j in range(planes // 2):
        pair = jnp.concatenate([modes[2 * j], modes[2 * j + 1]], axis=1)
        half = jnp.dot(pair, heights_two[...], preferred_element_type=jnp.float32).astype(jnp.bfloat16)
        full = jnp.dot(width[...], half, preferred_element_type=jnp.float32)
        solved[2 * j] = full[:, :heights]
        solved[2 * j + 1] = full[:, heights:]


def shards(previous, source, neighbor, depth, wall):
    pencils = lax.axis_size("pencil")
    _, planes, columns, heights = previous.shape
    boxes, _, segments = neighbor.shape
    segs = planes * segments // (planes * pencils)
    seglen = planes // segs
    xchips = boxes // ZCHIPS
    table = {name: jnp.asarray(value) for name, value in constants(planes, columns, heights).items()}
    lists = 2 * segs
    field = (planes, columns, heights)
    block = (seglen, heights)
    far = pl.BlockSpec(memory_space=pltpu.HBM)
    names = ("width", "height", "both", "turns", "rows", "modes")
    dma = pltpu.SemaphoreType.DMA
    modes = pl.pallas_call(
        functools.partial(front_kernel, pencils),
        out_shape=jax.ShapeDtypeStruct(field, jnp.bfloat16),
        in_specs=[far] * (5 + len(names)),
        out_specs=far,
        scratch_shapes=[
            pltpu.SMEM((2, segments, boxes), jnp.int32),
            pltpu.SMEM((2, segments, boxes), jnp.int32),
            pltpu.SMEM((2, planes), jnp.int32),
        ]
        + [pltpu.VMEM(table[name].shape, table[name].dtype) for name in names]
        + [
            pltpu.VMEM(field, jnp.bfloat16),
            pltpu.VMEM(field, jnp.bfloat16),
            pltpu.VMEM((2, planes, SLAB, heights), jnp.bfloat16),
            pltpu.VMEM(field, jnp.float32),
            pltpu.VMEM(field, jnp.float32),
            pltpu.VMEM(field, jnp.float32),
            pltpu.VMEM(field, jnp.bfloat16),
            pltpu.VMEM((2, 2, columns, heights), jnp.bfloat16),
            pltpu.VMEM((2, pencils - 1, columns, heights), jnp.bfloat16),
            pltpu.VMEM((2, columns, heights), jnp.float32),
            pltpu.VMEM((xchips, lists) + block, jnp.bfloat16),
            pltpu.VMEM((xchips, lists) + block, jnp.bfloat16),
            pltpu.VMEM((2, ZCHIPS - 1, lists) + block, jnp.bfloat16),
            pltpu.VMEM((ZCHIPS, lists) + block, jnp.bfloat16),
            pltpu.VMEM((ZCHIPS, lists) + block, jnp.bfloat16),
            pltpu.VMEM((4, planes, heights), jnp.float32),
            pltpu.VMEM((2, planes, heights), jnp.float32),
            pltpu.VMEM((2, planes, heights), jnp.int32),
            pltpu.VMEM((segs, 8, columns), jnp.float32),
            dma((2, LOADS)),
            dma((2,)),
            dma((3 + len(names),)),
            dma((columns // CHUNK,)),
            dma((2, xchips - 1)),
            dma((2, xchips - 1)),
            dma((2, ZCHIPS - 1)),
            dma((2, ZCHIPS - 1)),
            dma((2, pencils - 1)),
            dma((2, pencils - 1)),
        ],
        compiler_params=pltpu.CompilerParams(
            collective_id=0, has_side_effects=True, vmem_limit_bytes=67_043_328
        ),
        name="schwarz_modes",
    )(
        previous[0], source[0], neighbor.transpose(1, 2, 0), depth.transpose(1, 2, 0), wall[0],
        *[table[name] for name in names],
    )
    group = 8
    solved = pl.pallas_call(
        back_kernel,
        out_shape=jax.ShapeDtypeStruct(field, jnp.float32),
        grid=(planes // group,),
        in_specs=[
            pl.BlockSpec((group, columns, heights), lambda i: (i, 0, 0)),
            pl.BlockSpec((columns, columns), lambda i: (0, 0)),
            pl.BlockSpec((2 * heights, 2 * heights), lambda i: (0, 0)),
        ],
        out_specs=pl.BlockSpec((group, columns, heights), lambda i: (i, 0, 0)),
        name="back_to_cells",
    )(modes, table["width"], table["heights_two"])
    return solved[None]


def solution(mesh):
    placed = (
        P("box", "pencil", None, None),
        P("box", "pencil", None, None),
        P(),
        P(),
        P("box", None, "pencil"),
    )
    return jax.shard_map(
        shards,
        mesh=mesh,
        in_specs=placed,
        out_specs=P("box", "pencil", None, None),
        check_vma=False,
    )
```

```python
import functools

import jax
import jax.numpy as jnp
import ml_dtypes
import numpy as np
from jax import lax
from jax.experimental import pallas as pl
from jax.experimental.pallas import tpu as pltpu
from jax.sharding import PartitionSpec as P

W = 8
REFLECT = 0.6
TIMESTEP = 64.0
ZCHIPS = 8
SLAB = 16
CHUNK = 64
LOADS = 4

BF16 = ml_dtypes.bfloat16


def sine_table(length):
    ordinal = np.arange(length, dtype=np.float64) + 1.0
    phase_angle = np.pi * ordinal[:, None] * ordinal[None, :] / (length + 1.0)
    return np.sqrt(2.0 / (length + 1.0)) * np.sin(phase_angle)


def eigen_values(length):
    ordinal = np.arange(length, dtype=np.float64) + 1.0
    return 2.0 - 2.0 * np.cos(np.pi * ordinal / (length + 1.0))


def constants(planes, columns, heights):
    width = sine_table(columns)
    height = sine_table(heights).astype(BF16).astype(np.float64)
    gain = TIMESTEP * REFLECT
    faces = np.zeros((heights, heights))
    faces[0] = gain * height[0]
    faces[-1] = gain * height[-1]
    both = np.block([[height, height], [faces, np.zeros_like(faces)]])
    turn = gain * (np.outer(height[:, 0], height[0]) + np.outer(height[:, -1], height[-1]))
    nothing = np.zeros_like(turn)
    turns = np.block([[turn, nothing], [nothing, turn]])
    heights_two = np.block([[height, nothing], [nothing, height]])
    rows = np.concatenate([width[: W + 1], width[-W - 1 :]])
    rows = np.pad(rows, ((0, (-len(rows)) % 8), (0, 0)))
    rows = rows.reshape(len(rows), columns // CHUNK, CHUNK).transpose(1, 0, 2)
    slope = 2.0 + 1.0 / TIMESTEP + eigen_values(columns)[:, None] + eigen_values(heights)[None, :]
    ratio = 2.0 / (slope + np.sqrt(slope * slope - 4.0))
    weight = ratio / (1.0 - ratio * ratio) / TIMESTEP
    edge = np.broadcast_to(TIMESTEP * width[0][:, None], ratio.shape)
    modes = np.stack([ratio, planes * np.log(ratio), weight, edge])
    return dict(
        width=width.astype(BF16),
        height=height.astype(BF16),
        both=both.astype(BF16),
        turns=turns.astype(BF16),
        heights_two=heights_two.astype(BF16),
        rows=rows.astype(np.float32),
        modes=modes.astype(np.float32),
    )


def front_kernel(
    pencils, previous, source, neighbor_far, depth_far, wall_far, *more
):
    tables_far, (out, neighbor, depth, wall), more = more[:7], more[7:11], more[11:]
    tables, more = more[:7], more[7:]
    run_front(
        pencils, previous, source, (neighbor_far, depth_far, wall_far) + tables_far,
        (neighbor, depth, wall) + tables, *tables, neighbor, depth, wall, out, *more
    )


def run_front(
    pencils, previous, source, smalls_far, smalls, width, height, both, turns, heights_two, rowtab, modes,
    neighbor, depth, wall,
    out, prev, src, slab, right, force, carry, iterate, waves, inbox, own, gath0, gath1, packet, zbox0, zbox1,
    rows, ghost, walls, picks, load_sem, slab_sem, small_sem, out_sem, x_send, x_recv, z_send, z_recv,
    w_send, w_recv,
):
    gath = (gath0, gath1)
    zbox = (zbox0, zbox1)
    planes, columns, heights = prev.shape
    pencil = lax.axis_index("pencil")
    box = lax.axis_index("box")
    boxes = neighbor.shape[2]
    xchips = boxes // ZCHIPS
    cx = box // ZCHIPS
    cz = box % ZCHIPS
    seglen = planes * pencils // neighbor.shape[1]
    segs = planes // seglen
    gain = TIMESTEP * REFLECT
    step = planes // LOADS
    half = planes // 2

    x_peers = [(lax.rem(cx + k, xchips)) * ZCHIPS + cz for k in range(1, xchips)]
    z_peers = [cx * ZCHIPS + lax.rem(cz + k, ZCHIPS) for k in range(1, ZCHIPS)]
    w_peers = [lax.rem(pencil + k, pencils) for k in range(1, pencils)]

    barrier = pltpu.get_barrier_semaphore()
    for peer in x_peers + z_peers:
        pl.semaphore_signal(barrier, inc=1, device_id=(peer, pencil), device_id_type=pl.DeviceIdType.MESH)
    for peer in w_peers:
        pl.semaphore_signal(barrier, inc=1, device_id=(box, peer), device_id_type=pl.DeviceIdType.MESH)

    slab_loads = [
        pltpu.make_async_copy(previous.at[:, pl.ds(0, SLAB), :], slab.at[0], slab_sem.at[0]),
        pltpu.make_async_copy(previous.at[:, pl.ds(columns - SLAB, SLAB), :], slab.at[1], slab_sem.at[1]),
    ]
    small_loads = [
        pltpu.make_async_copy(there, here, small_sem.at[i])
        for i, (there, here) in enumerate(zip(smalls_far, smalls))
    ]
    for load in slab_loads + small_loads:
        load.start()

    def field_loads(c):
        part = pl.ds(c * step, step)
        return (
            pltpu.make_async_copy(previous.at[part], prev.at[part], load_sem.at[0, c]),
            pltpu.make_async_copy(source.at[part], src.at[part], load_sem.at[1, c]),
        )

    for c in range(LOADS):
        for load in field_loads(c):
            load.start()

    for load in small_loads:
        load.wait()
    lists = [(f, t) for f in range(2) for t in range(segs)]

    def search(b, found):
        return tuple(
            jnp.where(neighbor[f, pencil * segs + t, b] == box, depth[f, pencil * segs + t, b], d)
            for (f, t), d in zip(lists, found)
        )

    depths = lax.fori_loop(0, boxes, search, tuple(jnp.int32(1) for _ in lists))

    line = lax.broadcasted_iota(jnp.int32, (planes, heights), 0)
    for f in range(2):
        def mark(x, mask, f=f):
            return jnp.where(line == x, wall[f, x], mask)

        walls[f] = lax.fori_loop(0, planes, mark, jnp.zeros((planes, heights), jnp.int32))

    chunks = columns // CHUNK

    def chunk_at(c):
        return pl.ds(c * CHUNK, CHUNK)

    def x_copies(it):
        return [
            pltpu.make_async_remote_copy(
                gath[it].at[0], gath[it].at[k], x_send.at[it, k - 1], x_recv.at[it, k - 1],
                device_id=(x_peers[k - 1], pencil), device_id_type=pl.DeviceIdType.MESH,
            )
            for k in range(1, xchips)
        ]

    def z_copies(it):
        return [
            pltpu.make_async_remote_copy(
                packet.at[it, k - 1], zbox[it].at[k], z_send.at[it, k - 1], z_recv.at[it, k - 1],
                device_id=(z_peers[k - 1], pencil), device_id_type=pl.DeviceIdType.MESH,
            )
            for k in range(1, ZCHIPS)
        ]

    def w_copies(it, c):
        at = chunk_at(c)
        return [
            pltpu.make_async_remote_copy(
                waves.at[it, (pencil + k) // pencils, at], inbox.at[it, k - 1, at],
                w_send.at[it, c, k - 1], w_recv.at[it, c, k - 1],
                device_id=(box, w_peers[k - 1]), device_id_type=pl.DeviceIdType.MESH,
            )
            for k in range(1, pencils)
        ]

    def forward_margins(it):
        for k in range(ZCHIPS):
            reader = box if k == 0 else z_peers[k - 1]
            for j, (f, t) in enumerate(lists):
                donor = neighbor[f, pencil * segs + t, reader]
                block = gath[it][lax.rem(cx - donor // ZCHIPS + xchips, xchips), j]
                if k == 0:
                    zbox[it][0, j] = block
                else:
                    packet[it, k - 1, j] = block

    def imported(it, j):
        f, t = lists[j]
        donor = neighbor[f, pencil * segs + t, box]
        return zbox[it][lax.rem(cz - lax.rem(donor, ZCHIPS) + ZCHIPS, ZCHIPS), j].astype(jnp.float32)

    def imports(it, f):
        return jnp.concatenate([imported(it, f * segs + t) for t in range(segs)], axis=0)

    for load in slab_loads:
        load.wait()
    place = lax.broadcasted_iota(jnp.int32, (seglen, SLAB, heights), 1)
    for j, (f, t) in enumerate(lists):
        row = SLAB - 1 - depths[j] if f == 0 else depths[j]
        near = slab[1 - f, pl.ds(t * seglen, seglen)].astype(jnp.float32)
        gath0[0, j] = jnp.sum(jnp.where(place == row, near, 0.0), axis=1).astype(jnp.bfloat16)
    pl.semaphore_wait(barrier, len(x_peers) + len(z_peers) + len(w_peers))
    first_x = x_copies(0)
    for copy in first_x:
        copy.start()

    def transform(x, _):
        now = prev[x]
        total = (now.astype(jnp.float32) + src[x].astype(jnp.float32)).astype(jnp.bfloat16)
        turned = jnp.dot(
            width[...], jnp.concatenate([total, now], axis=1), preferred_element_type=jnp.float32
        ).astype(jnp.bfloat16)
        result = jnp.dot(turned, both[...], preferred_element_type=jnp.float32)
        right[x] = result[:, :heights]
        force[x] = result[:, heights:]
        return 0

    first_z = z_copies(0)
    for c in range(LOADS):
        for load in field_loads(c):
            load.wait()
        lax.fori_loop(c * step, (c + 1) * step, transform, 0, unroll=4)
        if c == LOADS // 2 - 1:
            for copy in first_x:
                copy.wait_recv()
            forward_margins(0)
            for copy in first_z:
                copy.start()

    at_start = jnp.where(pencil == 0, gain, 0.0).astype(jnp.float32)
    at_end = jnp.where(pencil == pencils - 1, gain, 0.0).astype(jnp.float32)
    for x, scale in ((0, at_start), (planes - 1, at_end)):
        turned = jnp.dot(width[...], prev[x], preferred_element_type=jnp.float32).astype(jnp.bfloat16)
        right[x] += scale * jnp.dot(turned, height[...], preferred_element_type=jnp.float32)

    for copy in first_z:
        copy.wait_recv()
    for f in range(2):
        wallrow = slab[f, :, 0 if f == 0 else SLAB - 1, :].astype(jnp.float32)
        value = jnp.where(walls[f] == 1, REFLECT * wallrow, imports(0, f))
        ghost[f] = jnp.dot(value.astype(jnp.bfloat16), height[...], preferred_element_type=jnp.float32)

    parity = lax.broadcasted_iota(jnp.int32, (CHUNK, heights), 0) % 2
    sign = jnp.where(parity == 0, 1.0, -1.0).astype(jnp.float32)
    near_power = (2 * pencil + 1).astype(jnp.float32)
    far_power = (2 * pencils - 1 - 2 * pencil).astype(jnp.float32)

    def sweep(it):
        def chunk(c):
            at = chunk_at(c)
            ratio = modes[0, at]
            edge = modes[3, at]

            def plane(i, carried):
                up, down, power = carried
                reach = ghost[0, pl.ds(i, 1), :] + sign * ghost[1, pl.ds(i, 1), :]
                value = right[i, at] + edge * reach
                right[i, at] = value
                return value + ratio * up, down + power * value, power * ratio

            zero = jnp.zeros((CHUNK, heights), jnp.float32)
            up, down, _ = lax.fori_loop(0, planes, plane, (zero, zero, zero + 1.0), unroll=4)
            log = modes[1, at]
            waves[it, 0, at] = (up - ratio * jnp.exp(log * near_power) * down).astype(jnp.bfloat16)
            waves[it, 1, at] = (down - ratio * jnp.exp(log * far_power) * up).astype(jnp.bfloat16)
            loop = ratio * ratio * jnp.exp(log * (2 * pencils - 1))
            own[0, at] = loop * up - ratio * jnp.exp(log * (near_power - 1.0)) * down
            own[1, at] = loop * down - ratio * jnp.exp(log * (far_power - 1.0)) * up
            for copy in w_copies(it, c):
                copy.start()

        for c in range(chunks):
            chunk(c)

    def solve(it, done):
        def chunk(c):
            at = chunk_at(c)
            for copy in w_copies(it, c):
                copy.wait_recv()
            ratio = modes[0, at]
            log = modes[1, at]
            weight = modes[2, at]
            decay = jnp.exp(log)
            low = jnp.zeros((CHUNK, heights), jnp.float32)
            high = low
            for k in range(pencils - 1, 0, -1):
                here = jnp.where(pencil >= k, 1.0, 0.0).astype(jnp.float32)
                low = here * inbox[it, k - 1, at].astype(jnp.float32) + decay * low
            for k in range(1, pencils):
                here = jnp.where(pencil >= k, 0.0, 1.0).astype(jnp.float32)
                high = here * inbox[it, k - 1, at].astype(jnp.float32) + decay * high
            start = low + own[0, at] - ratio * jnp.exp(log * near_power) * high
            end = high + own[1, at] - ratio * jnp.exp(log * far_power) * low

            def outer(j, carried):
                up, down = carried
                i, m = j, planes - 1 - j
                up = right[i, at] + ratio * up
                down = ratio * down
                carry[i, at] = up
                carry[m, at] = down
                return up, down + right[m, at]

            def inner(j, carried):
                up, down = carried
                i, m = j, planes - 1 - j
                up = right[i, at] + ratio * up
                down = ratio * down
                iterate[i, at] = (weight * (carry[i, at] + up)).astype(jnp.bfloat16)
                iterate[m, at] = (weight * (carry[m, at] + down)).astype(jnp.bfloat16)
                return up, down + right[m, at]

            carried = lax.fori_loop(0, half, outer, (start, end), unroll=4)
            lax.fori_loop(half, planes, inner, carried, unroll=4)
            done(c, at)

        for c in range(chunks):
            chunk(c)

    sweep(0)

    picks[...] = jnp.zeros_like(picks)
    wanted = [0, 2 * W + 1]
    for t in range(segs):
        wanted += [2 * W + 1 - depths[t], depths[segs + t]]
    for c in range(chunks):
        for q, row in enumerate(wanted):
            picks[c, pl.ds(q, 1), :] = rowtab[c, pl.ds(row, 1), :]
    rows[...] = jnp.zeros_like(rows)

    def pair_of(j, at=slice(None)):
        return jnp.concatenate([iterate[j, at], iterate[half + j, at]], axis=1)

    def take(c, at):
        lhs = picks[c].astype(jnp.bfloat16)
        for j in range(half):
            rows[j] += jnp.dot(lhs, pair_of(j, at), preferred_element_type=jnp.float32)

    solve(0, take)

    def row_at(q, t):
        return rows[:, q, t * heights : (t + 1) * heights]

    for j, (f, t) in enumerate(lists):
        gath1[0, j] = row_at(2 + 2 * t + f, t).astype(jnp.bfloat16)
    second_x = x_copies(1)
    for copy in second_x:
        copy.start()

    def faces(j, _):
        added = jnp.dot(pair_of(j), turns[...], preferred_element_type=jnp.float32)
        right[j] = force[j] + added[:, :heights]
        right[half + j] = force[half + j] + added[:, heights:]
        return 0

    lax.fori_loop(0, half // 2, faces, 0, unroll=4)
    for copy in second_x:
        copy.wait_recv()
    forward_margins(1)
    second_z = z_copies(1)
    for copy in second_z:
        copy.start()
    lax.fori_loop(half // 2, half, faces, 0, unroll=4)
    right[0] += at_start * iterate[0].astype(jnp.float32)
    right[planes - 1] += at_end * iterate[planes - 1].astype(jnp.float32)
    for copy in second_z:
        copy.wait_recv()
    for f in range(2):
        wallrows = jnp.concatenate([row_at(f, t) for t in range(segs)], axis=0)
        ghost[f] = jnp.where(walls[f] == 1, REFLECT * wallrows, imports(1, f))

    sweep(1)

    def to_cells(c, at):
        for j in range(half):
            cells = jnp.dot(pair_of(j, at), heights_two[...], preferred_element_type=jnp.float32)
            src[j, at] = cells[:, :heights].astype(jnp.bfloat16)
            src[half + j, at] = cells[:, heights:].astype(jnp.bfloat16)
        pltpu.make_async_copy(src.at[:, at, :], out.at[:, at, :], out_sem.at[c]).start()

    solve(1, to_cells)

    for c in range(chunks):
        at = chunk_at(c)
        pltpu.make_async_copy(src.at[:, at, :], out.at[:, at, :], out_sem.at[c]).wait()
        for it in range(2):
            for copy in w_copies(it, c):
                copy.wait_send()
    for copy in first_x + first_z + second_x + second_z:
        copy.wait_send()


def back_kernel(turned_far, width_far, solved_far, turned, width, solved, load_sem, width_sem, store_sem):
    planes, _, heights = turned.shape
    step = planes // LOADS

    def load(c):
        part = pl.ds(c * step, step)
        return pltpu.make_async_copy(turned_far.at[part], turned.at[part], load_sem.at[c])

    def store(c):
        part = pl.ds(c * step, step)
        return pltpu.make_async_copy(solved.at[part], solved_far.at[part], store_sem.at[c])

    table = pltpu.make_async_copy(width_far, width, width_sem)
    table.start()
    for c in range(LOADS):
        load(c).start()
    table.wait()

    def piece(c, _):
        load(c).wait()
        for j in range(0, step, 2):
            x = c * step + j
            pair = jnp.concatenate([turned[x], turned[x + 1]], axis=1)
            full = jnp.dot(width[...], pair, preferred_element_type=jnp.float32)
            solved[x] = full[:, :heights]
            solved[x + 1] = full[:, heights:]
        store(c).start()
        return 0

    lax.fori_loop(0, LOADS, piece, 0)
    for c in range(LOADS):
        store(c).wait()


def shards(previous, source, neighbor, depth, wall):
    pencils = lax.axis_size("pencil")
    _, planes, columns, heights = previous.shape
    boxes, _, segments = neighbor.shape
    segs = planes * segments // (planes * pencils)
    seglen = planes // segs
    xchips = boxes // ZCHIPS
    table = {name: jnp.asarray(value) for name, value in constants(planes, columns, heights).items()}
    lists = 2 * segs
    field = (planes, columns, heights)
    block = (seglen, heights)
    far = pl.BlockSpec(memory_space=pltpu.HBM)
    names = ("width", "height", "both", "turns", "heights_two", "rows", "modes")
    dma = pltpu.SemaphoreType.DMA
    turned = pl.pallas_call(
        functools.partial(front_kernel, pencils),
        out_shape=jax.ShapeDtypeStruct(field, jnp.bfloat16),
        in_specs=[far] * (5 + len(names)),
        out_specs=far,
        scratch_shapes=[
            pltpu.SMEM((2, segments, boxes), jnp.int32),
            pltpu.SMEM((2, segments, boxes), jnp.int32),
            pltpu.SMEM((2, planes), jnp.int32),
        ]
        + [pltpu.VMEM(table[name].shape, table[name].dtype) for name in names]
        + [
            pltpu.VMEM(field, jnp.bfloat16),
            pltpu.VMEM(field, jnp.bfloat16),
            pltpu.VMEM((2, planes, SLAB, heights), jnp.bfloat16),
            pltpu.VMEM(field, jnp.float32),
            pltpu.VMEM(field, jnp.float32),
            pltpu.VMEM(field, jnp.float32),
            pltpu.VMEM(field, jnp.bfloat16),
            pltpu.VMEM((2, 2, columns, heights), jnp.bfloat16),
            pltpu.VMEM((2, pencils - 1, columns, heights), jnp.bfloat16),
            pltpu.VMEM((2, columns, heights), jnp.float32),
            pltpu.VMEM((xchips, lists) + block, jnp.bfloat16),
            pltpu.VMEM((xchips, lists) + block, jnp.bfloat16),
            pltpu.VMEM((2, ZCHIPS - 1, lists) + block, jnp.bfloat16),
            pltpu.VMEM((ZCHIPS, lists) + block, jnp.bfloat16),
            pltpu.VMEM((ZCHIPS, lists) + block, jnp.bfloat16),
            pltpu.VMEM((planes // 2, 8, 2 * heights), jnp.float32),
            pltpu.VMEM((2, planes, heights), jnp.float32),
            pltpu.VMEM((2, planes, heights), jnp.int32),
            pltpu.VMEM((columns // CHUNK, 8, CHUNK), jnp.float32),
            dma((2, LOADS)),
            dma((2,)),
            dma((3 + len(names),)),
            dma((columns // CHUNK,)),
            dma((2, xchips - 1)),
            dma((2, xchips - 1)),
            dma((2, ZCHIPS - 1)),
            dma((2, ZCHIPS - 1)),
            dma((2, columns // CHUNK, pencils - 1)),
            dma((2, columns // CHUNK, pencils - 1)),
        ],
        compiler_params=pltpu.CompilerParams(
            collective_id=0, has_side_effects=True, vmem_limit_bytes=67_043_328
        ),
        name="schwarz_modes",
    )(
        previous[0], source[0], neighbor.transpose(1, 2, 0), depth.transpose(1, 2, 0), wall[0],
        *[table[name] for name in names],
    )
    solved = pl.pallas_call(
        back_kernel,
        out_shape=jax.ShapeDtypeStruct(field, jnp.float32),
        in_specs=[far, far],
        out_specs=far,
        scratch_shapes=[
            pltpu.VMEM(field, jnp.bfloat16),
            pltpu.VMEM((columns, columns), jnp.bfloat16),
            pltpu.VMEM(field, jnp.float32),
            dma((LOADS,)),
            dma(()),
            dma((LOADS,)),
        ],
        compiler_params=pltpu.CompilerParams(vmem_limit_bytes=67_043_328),
        name="back_to_cells",
    )(turned, table["width"])
    return solved[None]


def solution(mesh):
    placed = (
        P("box", "pencil", None, None),
        P("box", "pencil", None, None),
        P(),
        P(),
        P("box", None, "pencil"),
    )
    return jax.shard_map(
        shards,
        mesh=mesh,
        in_specs=placed,
        out_specs=P("box", "pencil", None, None),
        check_vma=False,
    )
```

```python
import functools

import jax
import jax.numpy as jnp
import ml_dtypes
import numpy as np
from jax import lax
from jax.experimental import pallas as pl
from jax.experimental.pallas import tpu as pltpu
from jax.sharding import PartitionSpec as P

W = 8
CORES = 2
REFLECT = 0.6
TIMESTEP = 64.0
ZCHIPS = 8
SLAB = 16
CHUNK = 64
LOADS = 4

BF16 = ml_dtypes.bfloat16


def sine_table(length):
    ordinal = np.arange(length, dtype=np.float64) + 1.0
    phase_angle = np.pi * ordinal[:, None] * ordinal[None, :] / (length + 1.0)
    return np.sqrt(2.0 / (length + 1.0)) * np.sin(phase_angle)


def eigen_values(length):
    ordinal = np.arange(length, dtype=np.float64) + 1.0
    return 2.0 - 2.0 * np.cos(np.pi * ordinal / (length + 1.0))


def constants(planes, columns, heights):
    width = sine_table(columns)
    height = sine_table(heights).astype(BF16).astype(np.float64)
    gain = TIMESTEP * REFLECT
    faces = np.zeros((heights, heights))
    faces[0] = gain * height[0]
    faces[-1] = gain * height[-1]
    both = np.block([[height, height], [faces, np.zeros_like(faces)]])
    turn = gain * (np.outer(height[:, 0], height[0]) + np.outer(height[:, -1], height[-1]))
    nothing = np.zeros_like(turn)
    turns = np.block([[turn, nothing], [nothing, turn]])
    heights_two = np.block([[height, nothing], [nothing, height]])
    rows = np.concatenate([width[: W + 1], width[-W - 1 :]])
    rows = np.pad(rows, ((0, (-len(rows)) % 8), (0, 0)))
    rows = rows.reshape(len(rows), columns // CHUNK, CHUNK).transpose(1, 0, 2)
    slope = 2.0 + 1.0 / TIMESTEP + eigen_values(columns)[:, None] + eigen_values(heights)[None, :]
    ratio = 2.0 / (slope + np.sqrt(slope * slope - 4.0))
    weight = ratio / (1.0 - ratio * ratio) / TIMESTEP
    edge = np.broadcast_to(TIMESTEP * width[0][:, None], ratio.shape)
    modes = np.stack([ratio, planes * np.log(ratio), weight, edge])
    return dict(
        width=width.astype(BF16),
        height=height.astype(BF16),
        both=both.astype(BF16),
        turns=turns.astype(BF16),
        heights_two=heights_two.astype(BF16),
        rows=rows.astype(np.float32),
        modes=modes.astype(np.float32),
    )


def front_kernel(
    pencils, previous, source, neighbor_far, depth_far, wall_far, *more
):
    tables_far, (out, neighbor, depth, wall), more = more[:7], more[7:11], more[11:]
    tables, more = more[:7], more[7:]
    run_front(
        pencils, previous, source, (neighbor_far, depth_far, wall_far) + tables_far,
        (neighbor, depth, wall) + tables, *tables, neighbor, depth, wall, out, *more
    )


def run_front(
    pencils, previous, source, smalls_far, smalls, width, height, both, turns, heights_two, rowtab, modes,
    neighbor, depth, wall,
    out, prev, src, slab, right, force, carry, iterate, waves, beside, pairs, inbox, ends, back, own, gath0, gath1, packet, zbox0, zbox1,
    rows, ghost, walls, picks, load_sem, slab_sem, small_sem, out_sem, x_send, x_recv, z_send, z_recv,
    near_send, near_recv, far_send, far_recv, back_send, back_recv,
):
    gath = (gath0, gath1)
    zbox = (zbox0, zbox1)
    planes, columns, heights = prev.shape
    pencil = lax.axis_index("pencil")
    box = lax.axis_index("box")
    boxes = neighbor.shape[2]
    xchips = boxes // ZCHIPS
    cx = box // ZCHIPS
    cz = box % ZCHIPS
    seglen = planes * pencils // neighbor.shape[1]
    segs = planes // seglen
    gain = TIMESTEP * REFLECT
    step = planes // LOADS
    half = planes // 2

    x_peers = [(lax.rem(cx + k, xchips)) * ZCHIPS + cz for k in range(1, xchips)]
    z_peers = [cx * ZCHIPS + lax.rem(cz + k, ZCHIPS) for k in range(1, ZCHIPS)]
    chips = pencils // CORES
    core = lax.rem(pencil, CORES)
    chip = pencil // CORES
    sibling = pencil + 1 - 2 * core
    far_peers = [lax.rem(chip + k, chips) * CORES + core for k in range(1, chips)]
    w_peers = [sibling] + far_peers
    pieces = columns // CORES // CHUNK

    barrier = pltpu.get_barrier_semaphore()
    for peer in x_peers + z_peers:
        pl.semaphore_signal(barrier, inc=1, device_id=(peer, pencil), device_id_type=pl.DeviceIdType.MESH)
    for peer in w_peers:
        pl.semaphore_signal(barrier, inc=1, device_id=(box, peer), device_id_type=pl.DeviceIdType.MESH)

    slab_loads = [
        pltpu.make_async_copy(previous.at[:, pl.ds(0, SLAB), :], slab.at[0], slab_sem.at[0]),
        pltpu.make_async_copy(previous.at[:, pl.ds(columns - SLAB, SLAB), :], slab.at[1], slab_sem.at[1]),
    ]
    small_loads = [
        pltpu.make_async_copy(there, here, small_sem.at[i])
        for i, (there, here) in enumerate(zip(smalls_far, smalls))
    ]
    for load in slab_loads + small_loads:
        load.start()

    def field_loads(c):
        part = pl.ds(c * step, step)
        return (
            pltpu.make_async_copy(previous.at[part], prev.at[part], load_sem.at[0, c]),
            pltpu.make_async_copy(source.at[part], src.at[part], load_sem.at[1, c]),
        )

    for c in range(LOADS):
        for load in field_loads(c):
            load.start()

    for load in small_loads[:2]:
        load.wait()
    lists = [(f, t) for f in range(2) for t in range(segs)]

    def search(b, found):
        return tuple(
            jnp.where(neighbor[f, pencil * segs + t, b] == box, depth[f, pencil * segs + t, b], d)
            for (f, t), d in zip(lists, found)
        )

    depths = lax.fori_loop(0, boxes, search, tuple(jnp.int32(1) for _ in lists), unroll=8)

    chunks = columns // CHUNK

    def place_of(s):
        half_of = 1 - core if s < pieces else core
        return half_of * pieces + s % pieces

    def chunk_at(s):
        return pl.ds(pl.multiple_of(place_of(s) * CHUNK, CHUNK), CHUNK)

    def piece_at(h):
        return pl.ds(h * CHUNK, CHUNK)

    def x_copies(it):
        return [
            pltpu.make_async_remote_copy(
                gath[it].at[0], gath[it].at[k], x_send.at[it, k - 1], x_recv.at[it, k - 1],
                device_id=(x_peers[k - 1], pencil), device_id_type=pl.DeviceIdType.MESH,
            )
            for k in range(1, xchips)
        ]

    def z_copies(it):
        return [
            pltpu.make_async_remote_copy(
                packet.at[it, k - 1], zbox[it].at[k], z_send.at[it, k - 1], z_recv.at[it, k - 1],
                device_id=(z_peers[k - 1], pencil), device_id_type=pl.DeviceIdType.MESH,
            )
            for k in range(1, ZCHIPS)
        ]

    def near_copy(it, s):
        at = piece_at(s)
        return pltpu.make_async_remote_copy(
            waves.at[it, :, at], beside.at[it, :, at], near_send.at[it, s], near_recv.at[it, s],
            device_id=(box, sibling), device_id_type=pl.DeviceIdType.MESH,
        )

    def far_copies(it, h):
        at = piece_at(h)
        return [
            pltpu.make_async_remote_copy(
                pairs.at[it, (chip + k) // chips, at], inbox.at[it, k - 1, at],
                far_send.at[it, h, k - 1], far_recv.at[it, h, k - 1],
                device_id=(box, far_peers[k - 1]), device_id_type=pl.DeviceIdType.MESH,
            )
            for k in range(1, chips)
        ]

    def back_copy(it, h):
        at = piece_at(h)
        return pltpu.make_async_remote_copy(
            ends.at[it, :, at], back.at[it, :, at], back_send.at[it, h], back_recv.at[it, h],
            device_id=(box, sibling), device_id_type=pl.DeviceIdType.MESH,
        )

    def forward_margins(it):
        for k in range(ZCHIPS):
            reader = box if k == 0 else z_peers[k - 1]
            for j, (f, t) in enumerate(lists):
                donor = neighbor[f, pencil * segs + t, reader]
                block = gath[it][lax.rem(cx - donor // ZCHIPS + xchips, xchips), j]
                if k == 0:
                    zbox[it][0, j] = block
                else:
                    packet[it, k - 1, j] = block

    def imported(it, j):
        f, t = lists[j]
        donor = neighbor[f, pencil * segs + t, box]
        return zbox[it][lax.rem(cz - lax.rem(donor, ZCHIPS) + ZCHIPS, ZCHIPS), j].astype(jnp.float32)

    def imports(it, f):
        return jnp.concatenate([imported(it, f * segs + t) for t in range(segs)], axis=0)

    for load in slab_loads:
        load.wait()
    place = lax.broadcasted_iota(jnp.int32, (seglen, SLAB, heights), 1)
    for j, (f, t) in enumerate(lists):
        row = SLAB - 1 - depths[j] if f == 0 else depths[j]
        near = slab[1 - f, pl.ds(t * seglen, seglen)].astype(jnp.float32)
        gath0[0, j] = jnp.sum(jnp.where(place == row, near, 0.0), axis=1).astype(jnp.bfloat16)
    pl.semaphore_wait(barrier, len(x_peers) + len(z_peers) + len(w_peers))
    first_x = x_copies(0)
    for copy in first_x:
        copy.start()

    for load in small_loads[2:]:
        load.wait()
    line = lax.broadcasted_iota(jnp.int32, (planes, heights), 0)
    for f in range(2):
        def mark(x, mask, f=f):
            return jnp.where(line == x, wall[f, x], mask)

        walls[f] = lax.fori_loop(0, planes, mark, jnp.zeros((planes, heights), jnp.int32))

    def transform(x, _):
        now = prev[x]
        total = (now.astype(jnp.float32) + src[x].astype(jnp.float32)).astype(jnp.bfloat16)
        turned = jnp.dot(
            width[...], jnp.concatenate([total, now], axis=1), preferred_element_type=jnp.float32
        ).astype(jnp.bfloat16)
        result = jnp.dot(turned, both[...], preferred_element_type=jnp.float32)
        right[x] = result[:, :heights]
        force[x] = result[:, heights:]
        return 0

    first_z = z_copies(0)
    for c in range(LOADS):
        for load in field_loads(c):
            load.wait()
        lax.fori_loop(c * step, (c + 1) * step, transform, 0, unroll=4)
        if c == LOADS // 2 - 1:
            for copy in first_x:
                copy.wait_recv()
            forward_margins(0)
            for copy in first_z:
                copy.start()

    at_start = jnp.where(pencil == 0, gain, 0.0).astype(jnp.float32)
    at_end = jnp.where(pencil == pencils - 1, gain, 0.0).astype(jnp.float32)
    for x, scale in ((0, at_start), (planes - 1, at_end)):
        turned = jnp.dot(width[...], prev[x], preferred_element_type=jnp.float32).astype(jnp.bfloat16)
        right[x] += scale * jnp.dot(turned, height[...], preferred_element_type=jnp.float32)

    for copy in first_z:
        copy.wait_recv()
    for f in range(2):
        wallrow = slab[f, :, 0 if f == 0 else SLAB - 1, :].astype(jnp.float32)
        value = jnp.where(walls[f] == 1, REFLECT * wallrow, imports(0, f))
        ghost[f] = jnp.dot(value.astype(jnp.bfloat16), height[...], preferred_element_type=jnp.float32)

    parity = lax.broadcasted_iota(jnp.int32, (CHUNK, heights), 0) % 2
    sign = jnp.where(parity == 0, 1.0, -1.0).astype(jnp.float32)
    near_power = (2 * pencil + 1).astype(jnp.float32)
    far_power = (2 * pencils - 1 - 2 * pencil).astype(jnp.float32)

    first_core = jnp.where(core == 0, 1.0, 0.0).astype(jnp.float32)
    last_core = 1.0 - first_core

    def join(it, h):
        at = chunk_at(pieces + h)
        near_copy(it, h).wait_recv()
        decay = jnp.exp(modes[1, at])
        mine = [waves[it, d, piece_at(pieces + h)].astype(jnp.float32) for d in range(2)]
        theirs = [beside[it, d, piece_at(h)].astype(jnp.float32) for d in range(2)]
        up = (first_core * decay + last_core) * mine[0] + (last_core * decay + first_core) * theirs[0]
        down = (last_core * decay + first_core) * mine[1] + (first_core * decay + last_core) * theirs[1]
        pairs[it, 0, piece_at(h)] = up.astype(jnp.bfloat16)
        pairs[it, 1, piece_at(h)] = down.astype(jnp.bfloat16)
        for copy in far_copies(it, h):
            copy.start()

    def reach_ends(it, h):
        for copy in far_copies(it, h):
            copy.wait_recv()
        decay = jnp.exp(CORES * modes[1, chunk_at(pieces + h)])
        low = jnp.zeros((CHUNK, heights), jnp.float32)
        high = low
        for k in range(chips - 1, 0, -1):
            here = jnp.where(chip >= k, 1.0, 0.0).astype(jnp.float32)
            low = here * inbox[it, k - 1, piece_at(h)].astype(jnp.float32) + decay * low
        for k in range(1, chips):
            here = jnp.where(chip >= k, 0.0, 1.0).astype(jnp.float32)
            high = here * inbox[it, k - 1, piece_at(h)].astype(jnp.float32) + decay * high
        ends[it, 0, piece_at(h)] = low.astype(jnp.bfloat16)
        ends[it, 1, piece_at(h)] = high.astype(jnp.bfloat16)
        back_copy(it, h).start()

    def sweep(it):
        def chunk(c):
            at = chunk_at(c)
            ratio = modes[0, at]
            edge = modes[3, at]

            def plane(i, carried):
                up, down, power = carried
                reach = ghost[0, pl.ds(i, 1), :] + sign * ghost[1, pl.ds(i, 1), :]
                value = right[i, at] + edge * reach
                right[i, at] = value
                return value + ratio * up, down + power * value, power * ratio

            zero = jnp.zeros((CHUNK, heights), jnp.float32)
            up, down, _ = lax.fori_loop(0, planes, plane, (zero, zero, zero + 1.0), unroll=4)
            log = modes[1, at]
            waves[it, 0, piece_at(c)] = (up - ratio * jnp.exp(log * near_power) * down).astype(jnp.bfloat16)
            waves[it, 1, piece_at(c)] = (down - ratio * jnp.exp(log * far_power) * up).astype(jnp.bfloat16)
            loop = ratio * ratio * jnp.exp(log * (2 * pencils - 1))
            own[0, at] = loop * up - ratio * jnp.exp(log * (near_power - 1.0)) * down
            own[1, at] = loop * down - ratio * jnp.exp(log * (far_power - 1.0)) * up
            near_copy(it, c).start()

        for c in range(chunks):
            chunk(c)
            if c >= pieces:
                join(it, c - pieces)
        for h in range(pieces):
            reach_ends(it, h)

    def solve(it, done):
        def chunk(c):
            at = chunk_at(c)
            ratio = modes[0, at]
            log = modes[1, at]
            weight = modes[2, at]
            decay = jnp.exp(log)
            if c >= pieces:
                outside = [ends[it, d, piece_at(c - pieces)].astype(jnp.float32) for d in range(2)]
            else:
                near_copy(it, c + pieces).wait_recv()
                back_copy(it, c).wait_recv()
                outside = [back[it, d, piece_at(c)].astype(jnp.float32) for d in range(2)]
            near = [beside[it, d, piece_at((c + pieces) % chunks)].astype(jnp.float32) for d in range(2)]
            low = last_core * near[0] + (last_core * decay + first_core) * outside[0]
            high = first_core * near[1] + (first_core * decay + last_core) * outside[1]
            start = low + own[0, at] - ratio * jnp.exp(log * near_power) * high
            end = high + own[1, at] - ratio * jnp.exp(log * far_power) * low

            def outer(j, carried):
                up, down = carried
                i, m = j, planes - 1 - j
                up = right[i, at] + ratio * up
                down = ratio * down
                carry[i, at] = up
                carry[m, at] = down
                return up, down + right[m, at]

            def inner(j, carried):
                up, down = carried
                i, m = j, planes - 1 - j
                up = right[i, at] + ratio * up
                down = ratio * down
                iterate[i, at] = (weight * (carry[i, at] + up)).astype(jnp.bfloat16)
                iterate[m, at] = (weight * (carry[m, at] + down)).astype(jnp.bfloat16)
                return up, down + right[m, at]

            carried = lax.fori_loop(0, half, outer, (start, end), unroll=4)
            lax.fori_loop(half, planes, inner, carried, unroll=4)
            done(c, at)

        for c in range(chunks):
            chunk((c + pieces) % chunks)

    sweep(0)

    picks[...] = jnp.zeros_like(picks)
    wanted = [0, 2 * W + 1]
    for t in range(segs):
        wanted += [2 * W + 1 - depths[t], depths[segs + t]]
    for c in range(chunks):
        for q, row in enumerate(wanted):
            picks[c, pl.ds(q, 1), :] = rowtab[c, pl.ds(row, 1), :]
    rows[...] = jnp.zeros_like(rows)

    def pair_of(j, at=slice(None)):
        return jnp.concatenate([iterate[j, at], iterate[half + j, at]], axis=1)

    def take(c, at):
        lhs = picks[place_of(c)].astype(jnp.bfloat16)
        for j in range(half):
            rows[j] += jnp.dot(lhs, pair_of(j, at), preferred_element_type=jnp.float32)

    solve(0, take)

    def row_at(q, t):
        return rows[:, q, t * heights : (t + 1) * heights]

    for j, (f, t) in enumerate(lists):
        gath1[0, j] = row_at(2 + 2 * t + f, t).astype(jnp.bfloat16)
    second_x = x_copies(1)
    for copy in second_x:
        copy.start()

    def faces(j, _):
        added = jnp.dot(pair_of(j), turns[...], preferred_element_type=jnp.float32)
        right[j] = force[j] + added[:, :heights]
        right[half + j] = force[half + j] + added[:, heights:]
        return 0

    lax.fori_loop(0, half // 2, faces, 0, unroll=4)
    for copy in second_x:
        copy.wait_recv()
    forward_margins(1)
    second_z = z_copies(1)
    for copy in second_z:
        copy.start()
    lax.fori_loop(half // 2, half, faces, 0, unroll=4)
    right[0] += at_start * iterate[0].astype(jnp.float32)
    right[planes - 1] += at_end * iterate[planes - 1].astype(jnp.float32)
    for copy in second_z:
        copy.wait_recv()
    for f in range(2):
        wallrows = jnp.concatenate([row_at(f, t) for t in range(segs)], axis=0)
        ghost[f] = jnp.where(walls[f] == 1, REFLECT * wallrows, imports(1, f))

    sweep(1)

    def to_cells(c, at):
        there = piece_at(c)
        for j in range(half):
            cells = jnp.dot(pair_of(j, at), heights_two[...], preferred_element_type=jnp.float32)
            src[j, there] = cells[:, :heights].astype(jnp.bfloat16)
            src[half + j, there] = cells[:, heights:].astype(jnp.bfloat16)
        pltpu.make_async_copy(src.at[:, there, :], out.at[:, there, :], out_sem.at[c]).start()

    solve(1, to_cells)

    for c in range(chunks):
        at = piece_at(c)
        pltpu.make_async_copy(src.at[:, at, :], out.at[:, at, :], out_sem.at[c]).wait()
        for it in range(2):
            near_copy(it, c).wait_send()
    for it in range(2):
        for h in range(pieces):
            for copy in far_copies(it, h) + [back_copy(it, h)]:
                copy.wait_send()
    for copy in first_x + first_z + second_x + second_z:
        copy.wait_send()


def back_kernel(turned_far, width_far, solved_far, turned, width, solved, load_sem, width_sem, store_sem):
    planes, columns, heights = turned.shape
    step = planes // LOADS
    core = lax.rem(lax.axis_index("pencil"), CORES)
    part_modes = columns // CORES
    low = pl.ds(pl.multiple_of((1 - core) * part_modes, part_modes), part_modes)
    high = pl.ds(pl.multiple_of(core * part_modes, part_modes), part_modes)

    def pair_at(rows, x):
        return jnp.concatenate([turned[x, rows], turned[x + 1, rows]], axis=1)

    def load(c):
        part = pl.ds(c * step, step)
        return pltpu.make_async_copy(turned_far.at[part], turned.at[part], load_sem.at[c])

    def store(c):
        part = pl.ds(c * step, step)
        return pltpu.make_async_copy(solved.at[part], solved_far.at[part], store_sem.at[c])

    table = pltpu.make_async_copy(width_far, width, width_sem)
    table.start()
    for c in range(LOADS):
        load(c).start()
    table.wait()

    def piece(c, _):
        load(c).wait()
        for j in range(0, step, 2):
            x = c * step + j
            pair = jnp.concatenate([pair_at(low, x), pair_at(high, x)], axis=0)
            full = jnp.dot(width[...], pair, preferred_element_type=jnp.float32)
            solved[x] = full[:, :heights]
            solved[x + 1] = full[:, heights:]
        store(c).start()
        return 0

    lax.fori_loop(0, LOADS, piece, 0)
    for c in range(LOADS):
        store(c).wait()


def shards(previous, source, neighbor, depth, wall):
    pencils = lax.axis_size("pencil")
    _, planes, columns, heights = previous.shape
    boxes, _, segments = neighbor.shape
    segs = planes * segments // (planes * pencils)
    seglen = planes // segs
    xchips = boxes // ZCHIPS
    table = {name: jnp.asarray(value) for name, value in constants(planes, columns, heights).items()}
    lists = 2 * segs
    field = (planes, columns, heights)
    block = (seglen, heights)
    far = pl.BlockSpec(memory_space=pltpu.HBM)
    names = ("width", "height", "both", "turns", "heights_two", "rows", "modes")
    dma = pltpu.SemaphoreType.DMA
    turned = pl.pallas_call(
        functools.partial(front_kernel, pencils),
        out_shape=jax.ShapeDtypeStruct(field, jnp.bfloat16),
        in_specs=[far] * (5 + len(names)),
        out_specs=far,
        scratch_shapes=[
            pltpu.SMEM((2, segments, boxes), jnp.int32),
            pltpu.SMEM((2, segments, boxes), jnp.int32),
            pltpu.SMEM((2, planes), jnp.int32),
        ]
        + [pltpu.VMEM(table[name].shape, table[name].dtype) for name in names]
        + [
            pltpu.VMEM(field, jnp.bfloat16),
            pltpu.VMEM(field, jnp.bfloat16),
            pltpu.VMEM((2, planes, SLAB, heights), jnp.bfloat16),
            pltpu.VMEM(field, jnp.float32),
            pltpu.VMEM(field, jnp.float32),
            pltpu.VMEM(field, jnp.float32),
            pltpu.VMEM(field, jnp.bfloat16),
            pltpu.VMEM((2, 2, columns, heights), jnp.bfloat16),
            pltpu.VMEM((2, 2, columns, heights), jnp.bfloat16),
            pltpu.VMEM((2, 2, columns // CORES, heights), jnp.bfloat16),
            pltpu.VMEM((2, pencils // CORES - 1, columns // CORES, heights), jnp.bfloat16),
            pltpu.VMEM((2, 2, columns // CORES, heights), jnp.bfloat16),
            pltpu.VMEM((2, 2, columns // CORES, heights), jnp.bfloat16),
            pltpu.VMEM((2, columns, heights), jnp.float32),
            pltpu.VMEM((xchips, lists) + block, jnp.bfloat16),
            pltpu.VMEM((xchips, lists) + block, jnp.bfloat16),
            pltpu.VMEM((2, ZCHIPS - 1, lists) + block, jnp.bfloat16),
            pltpu.VMEM((ZCHIPS, lists) + block, jnp.bfloat16),
            pltpu.VMEM((ZCHIPS, lists) + block, jnp.bfloat16),
            pltpu.VMEM((planes // 2, 8, 2 * heights), jnp.float32),
            pltpu.VMEM((2, planes, heights), jnp.float32),
            pltpu.VMEM((2, planes, heights), jnp.int32),
            pltpu.VMEM((columns // CHUNK, 8, CHUNK), jnp.float32),
            dma((2, LOADS)),
            dma((2,)),
            dma((3 + len(names),)),
            dma((columns // CHUNK,)),
            dma((2, xchips - 1)),
            dma((2, xchips - 1)),
            dma((2, ZCHIPS - 1)),
            dma((2, ZCHIPS - 1)),
            dma((2, columns // CHUNK)),
            dma((2, columns // CHUNK)),
            dma((2, columns // CORES // CHUNK, pencils // CORES - 1)),
            dma((2, columns // CORES // CHUNK, pencils // CORES - 1)),
            dma((2, columns // CORES // CHUNK)),
            dma((2, columns // CORES // CHUNK)),
        ],
        compiler_params=pltpu.CompilerParams(
            collective_id=0, has_side_effects=True, vmem_limit_bytes=67_043_328
        ),
        name="schwarz_modes",
    )(
        previous[0], source[0], neighbor.transpose(1, 2, 0), depth.transpose(1, 2, 0), wall[0],
        *[table[name] for name in names],
    )
    solved = pl.pallas_call(
        back_kernel,
        out_shape=jax.ShapeDtypeStruct(field, jnp.float32),
        in_specs=[far, far],
        out_specs=far,
        scratch_shapes=[
            pltpu.VMEM(field, jnp.bfloat16),
            pltpu.VMEM((columns, columns), jnp.bfloat16),
            pltpu.VMEM(field, jnp.float32),
            dma((LOADS,)),
            dma(()),
            dma((LOADS,)),
        ],
        compiler_params=pltpu.CompilerParams(vmem_limit_bytes=67_043_328),
        name="back_to_cells",
    )(turned, table["width"])
    return solved[None]


def solution(mesh):
    placed = (
        P("box", "pencil", None, None),
        P("box", "pencil", None, None),
        P(),
        P(),
        P("box", None, "pencil"),
    )
    return jax.shard_map(
        shards,
        mesh=mesh,
        in_specs=placed,
        out_specs=P("box", "pencil", None, None),
        check_vma=False,
    )
```
